256 devices in a mesh: ctx: 64 (over z, x, core), head: 4 (over y).
Axes of the slice: x: 4, y: 4, z: 8, core: 2. Of those that a mesh axis runs over, the one named last changes fastest.
Arguments:
- queries: bfloat16 [65536, 1024], P('ctx', 'head'), may hold values from -6 to 6
- keys: bfloat16 [65536, 1024], P('ctx', 'head'), may hold values from -6 to 6
- values: bfloat16 [65536, 1024], P('ctx', 'head'), may hold values from -6 to 6
- level_index: int32 [65536], P('ctx'), may hold values from 0 to 15
- level_table: float32 [16, 8, 11], P(None, 'head'), may hold values from 0.2 to 2
- head_gain: float32 [1024], P('head'), may hold values from 0.5 to 1.5
- residual: bfloat16 [65536, 1024], P(('ctx', 'head')), may hold values from -6 to 6
- w_out: bfloat16 [1024, 1024], replicated, may hold values from -0.1875 to 0.1875
- norm_gain: float32 [1024], replicated, may hold values from 0.5 to 1.5
- w_qkv: bfloat16 [1024, 3072], replicated, may hold values from -8 to 8
- windows: int32 [8], replicated, may hold values from 64 to 256, as said below
Outputs:
- hidden: bfloat16 [65536, 1024], P(('ctx', 'head'))
- attended: bfloat16 [65536, 1024], P('ctx', 'head')
The draws below stay inside these ranges and needn't reach their ends.
Inputs may be any that keep to these rules, and one draw needn't show every extreme that they name: `windows`: each head's key window; some head's window is exactly 256 in every draw.
All inputs are finite; a program needn't handle non-finite values.
Results may differ from the reference program's by a relative error of at most 0.014.
Values may be sent and summed in bfloat16 or wider, within the bound.
No kernel may reach another device: no remote copies, remote signals or barrier semaphores. Data moves between devices by JAX's collectives and lax.ppermute only.
A program may use at most 128 MiB of HBM per device.

```python
import math
import jax
import jax.numpy as jnp
from jax import lax

D = 1024
H = 8
DH = 128
STRETCH = 64
WINDOW = 256
NTAB = 16
TOK_DEV = 1024
TOKENS = 65536
LEVELS = 11
N_CTX = 64


def draw_windows(key, part):
    first_key, second_key = jax.random.split(jax.random.fold_in(key, 11))
    drawn = jax.random.randint(first_key, (H,), WINDOW // 4, WINDOW + 1, dtype=jnp.int32)
    chosen = jax.random.randint(second_key, (), 0, H, dtype=jnp.int32)
    return jnp.where(jnp.arange(H, dtype=jnp.int32) == chosen, WINDOW, drawn).astype(jnp.int32)


def draw_w_qkv(key, part):
    base_key = jax.random.fold_in(jax.random.fold_in(key, 23), 0)
    base = jax.random.normal(base_key, (D, 3, H, DH), jnp.float32) * D ** (-0.5)
    return jnp.clip(base, -8.0, 8.0).reshape(D, 3 * D).astype(jnp.bfloat16)


def set_ends(values, own_key, low, high):
    shape = values.shape
    place = [jax.random.randint(jax.random.fold_in(own_key, axis), (), 0, shape[axis]) for axis in range(len(shape))]
    values = values.at[tuple(place)].set(low)
    longest = shape.index(max(shape))
    place[longest] = (place[longest] + 1) % shape[longest]
    return values.at[tuple(place)].set(high)


def steps_of(stream_key, extent, pieces, smallest, high):
    level, own = 1.0, jax.random.fold_in(stream_key, 6)
    for position, parts in pieces:
        steps = jnp.exp(jax.random.uniform(jax.random.fold_in(own, position), (parts,), jnp.float32, smallest / len(pieces), high / len(pieces)))
        level = level * jnp.repeat(steps, extent[position] // parts).reshape([-1 if axis == position else 1 for axis in range(len(extent))])
    return level


def normal_values(rng, shape, deviation, bound, cuts=(), held_as=jnp.bfloat16):
    values = deviation * jax.random.normal(rng, shape, jnp.float32)
    if cuts:
        values = values * steps_of(rng, shape, cuts, -0.22, 0.18)
    return jnp.clip(values, -bound, bound).astype(held_as)


def setup_inputs(seed: int = 0) -> dict:
    key_list = jax.random.split(jax.random.key(seed), 12)
    queries = normal_values(key_list[0], (TOKENS, D), 1.0, 6.0, ((0, 64), (1, 4)))
    keys = normal_values(key_list[1], (TOKENS, D), 1.0, 6.0, ((0, 64), (1, 4)))
    values = normal_values(key_list[2], (TOKENS, D), 1.0, 6.0, ((0, 64), (1, 4)))
    level_index = set_ends(jax.random.randint(key_list[3], (TOKENS,), 0, NTAB), jax.random.fold_in(key_list[3], 1), 0, NTAB - 1).astype(jnp.int32)
    level_table = jnp.clip(jnp.exp(math.log(2.0) - 2.3025851 * jax.random.uniform(key_list[4], (NTAB, H, LEVELS), jnp.float32) ** steps_of(key_list[4], (NTAB, H, LEVELS), ((1, 4),), -0.2, 0.2)), 0.2, 2.0)
    head_gain = jnp.clip(1.0 + 0.1 * jax.random.normal(key_list[5], (D,), jnp.float32), 0.5, 1.5)
    residual = normal_values(key_list[6], (TOKENS, D), 1.0, 6.0, ((0, 256),))
    w_out = normal_values(key_list[7], (D, D), D ** -0.5, 0.1875)
    norm_gain = jnp.clip(1.0 + 0.1 * jax.random.normal(key_list[8], (D,), jnp.float32), 0.5, 1.5)
    w_qkv = draw_w_qkv(jax.random.fold_in(key_list[11], 71), 0)
    windows = draw_windows(jax.random.fold_in(key_list[11], 71), 0)
    return {"queries": queries, "keys": keys, "values": values, "level_index": level_index, "level_table": level_table, "head_gain": head_gain, "residual": residual, "w_out": w_out, "norm_gain": norm_gain, "w_qkv": w_qkv, "windows": windows}


EPSILON = 1e-05
PRECISE = lax.Precision.HIGHEST

def rounded(array):
    return lax.optimization_barrier(array.astype(jnp.bfloat16)).astype(jnp.float32)

def reference(queries, keys, values, level_index, level_table, head_gain, residual, w_out, norm_gain, w_qkv, windows):
    stretch_count = TOKENS // STRETCH
    bit_count = LEVELS - 1
    query_all = queries.reshape(stretch_count, STRETCH, H, DH)
    key_all = keys.reshape(stretch_count, STRETCH, H, DH)
    value_all = values.reshape(stretch_count, STRETCH, H, DH)
    level_weight = level_table[level_index].reshape(stretch_count, STRETCH, H, LEVELS)
    level_rates = jnp.array([STRETCH ** (-0.5)] + [(STRETCH * 2 ** level_bit) ** (-0.5) for level_bit in range(bit_count)], jnp.float32)
    causal = jnp.arange(STRETCH, dtype=jnp.int32)[:, None] >= jnp.arange(STRETCH, dtype=jnp.int32)[None, :]
    bit_numbers = jnp.arange(bit_count, dtype=jnp.int32)
    spans = 2 ** bit_numbers

    def advance(carry, inputs):
        partial_sums, finished = carry
        stretch_index, query_stretch, key_stretch, value_stretch, weight_stretch = inputs
        query_f = query_stretch.astype(jnp.float32)
        key_f = key_stretch.astype(jnp.float32)
        value_f = value_stretch.astype(jnp.float32)
        scores = jnp.einsum('thd,shd->hts', query_f, key_f)
        scores = rounded(jnp.where(causal[None], scores, 0.0))
        inside = jnp.einsum('hts,shd->thd', scores, value_f)
        combined = weight_stretch[:, :, 0][:, :, None] * level_rates[0] * inside
        active = (stretch_index // spans % 2).astype(jnp.float32)
        read_state = rounded(finished) * active[:, None, None, None]
        far_terms = jnp.einsum('thd,bhde->tbhe', query_f, read_state, precision=PRECISE)
        combined = combined + jnp.einsum('tbhe,thb->the', far_terms, weight_stretch[:, :, 1:] * level_rates[1:], precision=PRECISE)
        stretch_state = jnp.einsum('thd,the->hde', key_f, value_f, precision=PRECISE)
        partial_sums = partial_sums + stretch_state[None]
        closing = (stretch_index + 1) % spans == 0
        finished = jnp.where(closing[:, None, None, None], partial_sums, finished)
        partial_sums = jnp.where(closing[:, None, None, None], 0.0, partial_sums)
        return ((partial_sums, finished), combined)
    empty_states = jnp.zeros((bit_count, H, DH, DH), jnp.float32)
    stretch_ids = jnp.arange(stretch_count, dtype=jnp.int32)
    carry_out, heads_raw = lax.scan(advance, (empty_states, empty_states), (stretch_ids, query_all, key_all, value_all, level_weight))
    heads_raw = heads_raw.reshape(TOKENS, H, DH)
    mean_square = lax.optimization_barrier(jnp.mean(heads_raw * heads_raw, -1, keepdims=True))
    heads_out = (heads_raw * lax.rsqrt(mean_square + EPSILON) * head_gain.reshape(H, DH)).astype(jnp.bfloat16).reshape(TOKENS, D)
    projected = jnp.dot(heads_out, w_out, preferred_element_type=jnp.float32)
    hidden = (residual.astype(jnp.float32) + projected).astype(jnp.bfloat16)
    hidden_f = hidden.astype(jnp.float32)
    normed = (hidden_f * lax.rsqrt(lax.optimization_barrier(jnp.mean(hidden_f * hidden_f, -1, keepdims=True)) + EPSILON) * norm_gain).astype(jnp.bfloat16)
    projected_qkv = jnp.dot(normed, w_qkv, preferred_element_type=jnp.float32).astype(jnp.bfloat16).reshape(TOKENS, 3, H, DH)
    padding = jnp.zeros((WINDOW, H, DH), jnp.bfloat16)
    query_rows = projected_qkv[:, 0]
    key_padded = jnp.concatenate([padding, projected_qkv[:, 1]], 0)
    value_padded = jnp.concatenate([padding, projected_qkv[:, 2]], 0)

    def attend(start):
        query_block = lax.dynamic_slice_in_dim(query_rows, start, TOK_DEV, 0).astype(jnp.float32)
        key_block = lax.dynamic_slice_in_dim(key_padded, start, TOK_DEV + WINDOW, 0).astype(jnp.float32)
        value_block = lax.dynamic_slice_in_dim(value_padded, start, TOK_DEV + WINDOW, 0).astype(jnp.float32)
        scores = jnp.einsum('qhd,khd->hqk', query_block, key_block) * DH ** (-0.5)
        query_pos = start + jnp.arange(TOK_DEV, dtype=jnp.int32)
        key_pos = start - WINDOW + jnp.arange(TOK_DEV + WINDOW, dtype=jnp.int32)
        distance = query_pos[:, None] - key_pos[None, :]
        allowed = (distance >= 0)[None] & (distance < windows[:, None, None]) & (key_pos >= 0)[None, None, :]
        scores = jnp.where(allowed, scores, -1e+30)
        row_max = lax.optimization_barrier(jnp.max(scores, -1, keepdims=True))
        weights = jnp.exp(scores - row_max)
        probs = rounded(weights / lax.optimization_barrier(jnp.sum(weights, -1, keepdims=True)))
        block_out = jnp.einsum('hqk,khd->qhd', probs, value_block)
        return block_out.astype(jnp.bfloat16).reshape(TOK_DEV, D)
    starts = jnp.arange(N_CTX, dtype=jnp.int32) * TOK_DEV
    attended = lax.map(attend, starts).reshape(TOKENS, D)
    return (hidden, attended)
```

```python
import jax
import jax.numpy as jnp
from jax import lax
from jax.experimental import pallas as pl
from jax.experimental.pallas import tpu as pltpu
from jax.sharding import PartitionSpec as P

STRETCH = 64
WINDOW = 256
EPSILON = 1e-05
BLOCK = 256
DH = 128
CTX_ROUTES = (1, 2, 6, 8, 16, 48)

VMEM = pl.BlockSpec(memory_space=pltpu.VMEM)
SMEM = pl.BlockSpec(memory_space=pltpu.SMEM)
F32 = jnp.float32
BF16 = jnp.bfloat16


def dot(a, b, dims=((1,), (0,))):
    return lax.dot_general(a, b, (dims, ((), ())), preferred_element_type=F32)


def call(kernel, outs, args, specs, flops, nbytes, name, vmem=24):
    return pl.pallas_call(
        kernel,
        out_shape=[jax.ShapeDtypeStruct(s, d) for s, d in outs],
        in_specs=specs,
        out_specs=[VMEM] * len(outs),
        compiler_params=pltpu.CompilerParams(vmem_limit_bytes=vmem * 2**20),
        cost_estimate=pl.CostEstimate(flops=flops, bytes_accessed=nbytes, transcendentals=0),
        name=name,
    )(*args)


def state_kernel(k_ref, v_ref, state_ref, send_ref, read_ref):
    heads = state_ref.shape[0] // DH
    for h in range(heads):
        lanes = slice(h * DH, (h + 1) * DH)
        blocks = []
        for i in range(k_ref.shape[0] // BLOCK):
            rows = slice(i * BLOCK, (i + 1) * BLOCK)
            blocks.append(dot(k_ref[rows, lanes], v_ref[rows, lanes], ((0,), (0,))))
        half = blocks[0] + blocks[1]
        total = half + (blocks[2] + blocks[3])
        state_ref[lanes, :] = total
        send_ref[lanes, :] = total.astype(BF16)
        read_ref[0, lanes, :] = blocks[0].astype(BF16)
        read_ref[1, lanes, :] = blocks[2].astype(BF16)
        read_ref[2, lanes, :] = half.astype(BF16)


def weight_kernel(index_ref, table_ref, weight_ref):
    table = table_ref[...]
    high = table.astype(BF16)
    rest = table - high.astype(F32)
    middle = rest.astype(BF16)
    low = (rest - middle.astype(F32)).astype(BF16)
    pieces = jnp.concatenate([high, middle, low], 0)
    index = index_ref[...]
    rows = lax.broadcasted_iota(jnp.int32, (table.shape[0], index.shape[1]), 0)
    onehot = (rows == index).astype(F32).astype(BF16)
    weight_ref[...] = dot(jnp.concatenate([onehot] * 3, 0), pieces, ((0,), (0,)))


def local_kernel(levels, q_ref, k_ref, v_ref, read_ref, weight_ref, run_ref):
    heads = run_ref.shape[1] // DH
    t = lax.broadcasted_iota(jnp.int32, (BLOCK, BLOCK), 0)
    s = lax.broadcasted_iota(jnp.int32, (BLOCK, BLOCK), 1)
    same = t // STRETCH == s // STRETCH
    pair = t // (2 * STRETCH) == s // (2 * STRETCH)
    causal = t >= s
    for i in range(q_ref.shape[0] // BLOCK):
        rows = slice(i * BLOCK, (i + 1) * BLOCK)
        for h in range(heads):
            lanes = slice(h * DH, (h + 1) * DH)
            q = q_ref[rows, lanes]

            def weight(level):
                c = h * levels + level
                return weight_ref[rows, c : c + 1]

            scores = dot(q, k_ref[rows, lanes], ((1,), (1,)))
            scale = jnp.where(same, weight(0), jnp.where(pair, weight(1), weight(2)))
            mixed = jnp.where(causal, scores * scale, 0.0).astype(BF16)
            out = dot(mixed, v_ref[rows, lanes])
            if i % 2:
                out += weight(3) * dot(q, read_ref[i // 2, lanes, :])
            if i >= 2:
                out += weight(4) * dot(q, read_ref[2, lanes, :])
            run_ref[rows, lanes] = out


def far_sum(first, levels, rows, h, q_ref, weight_ref, reads):
    lanes = slice(h * DH, (h + 1) * DH)
    q = q_ref[rows, lanes]
    total = None
    for j, read in enumerate(reads):
        c = h * levels + first + j
        term = weight_ref[rows, c : c + 1] * dot(q, read[lanes, :])
        total = term if total is None else total + term
    return total


def far_kernel(first, levels, run_ref, q_ref, weight_ref, *rest):
    *reads, out_ref = rest
    for i in range(q_ref.shape[0] // BLOCK):
        rows = slice(i * BLOCK, (i + 1) * BLOCK)
        for h in range(out_ref.shape[1] // DH):
            lanes = slice(h * DH, (h + 1) * DH)
            out_ref[rows, lanes] = run_ref[rows, lanes] + far_sum(
                first, levels, rows, h, q_ref, weight_ref, reads
            )


def finish_kernel(first, levels, start, run_ref, q_ref, weight_ref, gain_ref, *rest):
    *reads, out_ref = rest
    for i in range(out_ref.shape[0] // BLOCK):
        rows = slice(start + i * BLOCK, start + (i + 1) * BLOCK)
        for h in range(out_ref.shape[1] // DH):
            lanes = slice(h * DH, (h + 1) * DH)
            total = run_ref[rows, lanes] + far_sum(
                first, levels, rows, h, q_ref, weight_ref, reads
            )
            square = jnp.mean(total * total, -1, keepdims=True)
            scaled = total * lax.rsqrt(square + EPSILON) * gain_ref[:, lanes]
            out_ref[i * BLOCK : (i + 1) * BLOCK, lanes] = scaled.astype(BF16)


def project_kernel(
    chunk,
    info_ref,
    own_ref,
    left_ref,
    right_ref,
    far_left_ref,
    far_right_ref,
    res0_ref,
    res1_ref,
    res2_ref,
    res3_ref,
    w_out_ref,
    gain_ref,
    w_q_ref,
    w_k_ref,
    w_v_ref,
    q_ref,
    k_ref,
    v_ref,
    hidden_ref,
):
    me = info_ref[0]
    group = 4
    width = own_ref.shape[1]

    def rows_of(owner):
        return w_out_ref[pl.ds(pl.multiple_of(owner * width, width), width), :]

    for j in range(own_ref.shape[0] // BLOCK):
        rows = slice(j * BLOCK, (j + 1) * BLOCK)
        block = chunk * (own_ref.shape[0] // BLOCK) + j
        distance = lax.rem(me - block + group, group)
        far_ref = far_left_ref if j == 0 else far_right_ref
        total = dot(own_ref[rows, :], rows_of(me))
        total += dot(left_ref[rows, :], rows_of(lax.rem(me + 3, group)))
        total += dot(right_ref[rows, :], rows_of(lax.rem(me + 1, group)))
        total += dot(far_ref[...], rows_of(lax.rem(me + 2, group)))
        res = jnp.where(
            distance < 2,
            jnp.where(distance == 0, res0_ref[...], res1_ref[...]),
            jnp.where(distance == 2, res2_ref[...], res3_ref[...]),
        )
        hidden = (res.astype(F32) + total).astype(BF16)

        @pl.when(distance == 0)
        def _(hidden=hidden):
            hidden_ref[...] = hidden

        wide = hidden.astype(F32)
        square = jnp.mean(wide * wide, -1, keepdims=True)
        normed = (wide * lax.rsqrt(square + EPSILON) * gain_ref[...]).astype(BF16)
        q_ref[rows, :] = dot(normed, w_q_ref[...]).astype(BF16)
        k_ref[rows, :] = dot(normed, w_k_ref[...]).astype(BF16)
        v_ref[rows, :] = dot(normed, w_v_ref[...]).astype(BF16)


def attend_kernel(halo, info_ref, q_ref, k_ref, v_ref, k_before_ref, v_before_ref, out_ref):
    scale = DH ** (-0.5)
    t = lax.broadcasted_iota(jnp.int32, (BLOCK, 2 * BLOCK), 0) + BLOCK
    s = lax.broadcasted_iota(jnp.int32, (BLOCK, 2 * BLOCK), 1)
    distance = t - s
    for h in range(out_ref.shape[1] // DH):
        lanes = slice(h * DH, (h + 1) * DH)
        window = info_ref[1 + h]
        allowed = (distance >= 0) & (distance < window)
        for i in range(out_ref.shape[0] // BLOCK):
            rows = slice(i * BLOCK, (i + 1) * BLOCK)
            if i == 0:
                k_before = k_before_ref[-BLOCK:, lanes]
                v_before = v_before_ref[-BLOCK:, lanes]
            else:
                k_before = k_ref[(i - 1) * BLOCK : i * BLOCK, lanes]
                v_before = v_ref[(i - 1) * BLOCK : i * BLOCK, lanes]
            k = jnp.concatenate([k_before, k_ref[rows, lanes]], 0)
            v = jnp.concatenate([v_before, v_ref[rows, lanes]], 0)
            valid = allowed
            if halo and i == 0:
                valid = allowed & ((s >= BLOCK) | (info_ref[3] > 0))
            scores = dot(q_ref[rows, lanes], k, ((1,), (1,))) * scale
            scores = jnp.where(valid, scores, -1e30)
            weights = jnp.exp(scores - jnp.max(scores, -1, keepdims=True))
            total = jnp.sum(weights, -1, keepdims=True)
            probs = (weights / total).astype(BF16)
            out_ref[rows, lanes] = dot(probs, v).astype(BF16)


def shift(array, axis, route):
    size = lax.axis_size(axis)
    pairs = [(i, route(i)) for i in range(size) if 0 <= route(i) < size]
    return lax.ppermute(array, axis, pairs)


def per_device(
    queries,
    keys,
    values,
    level_index,
    level_table,
    head_gain,
    residual,
    w_out,
    norm_gain,
    w_qkv,
    windows,
):
    tokens, width = queries.shape
    heads = width // DH
    levels = level_table.shape[2]
    group = lax.axis_size("head")
    model = residual.shape[1]
    head = lax.axis_index("head")
    position = lax.axis_index("ctx")
    info = jnp.concatenate(
        [
            head[None],
            lax.dynamic_slice_in_dim(windows, head * heads, heads),
            position[None],
        ]
    ).astype(jnp.int32)
    rates = jnp.array(
        [STRETCH ** (-0.5)] + [(STRETCH * 2**b) ** (-0.5) for b in range(levels - 1)], F32
    )
    table = (level_table * rates).reshape(level_table.shape[0], heads * levels)
    table = jnp.pad(table, ((0, 0), (0, DH - heads * levels)))
    gain = head_gain.reshape(1, width)

    state, send, near = call(
        state_kernel,
        [((width, DH), F32), ((width, DH), BF16), ((3, width, DH), BF16)],
        (keys, values),
        [VMEM] * 2,
        2 * tokens * width * DH,
        2**20,
        "state",
    )
    (weight,) = call(
        weight_kernel,
        [((tokens, DH), F32)],
        (level_index.reshape(1, tokens), table),
        [VMEM] * 2,
        2 * tokens * DH * DH,
        2**20,
        "weight",
    )
    (run,) = call(
        lambda *refs: local_kernel(levels, *refs),
        [((tokens, width), F32)],
        (queries, keys, values, near, weight),
        [VMEM] * 5,
        2 * tokens * width * 1024,
        2**22,
        "local",
    )

    reads = []
    for b, route in enumerate(CTX_ROUTES):
        other = shift(send, "ctx", lambda i, r=route: i ^ r)
        bit = (position >> b) & 1
        reads.append(other * bit.astype(BF16))
        state = state + other.astype(F32)
        send = state.astype(BF16)

    res = [residual] + [
        shift(residual, "head", lambda i, d=d: (i + d) % group) for d in range(1, group)
    ]
    local_levels = levels - len(reads)
    early = len(reads) - 2
    (run,) = call(
        lambda *refs: far_kernel(local_levels, levels, *refs),
        [((tokens, width), F32)],
        (run, queries, weight, *reads[:early]),
        [VMEM] * (3 + early),
        2 * tokens * width * DH * early,
        2**22,
        "far",
    )
    chunk_rows = tokens // 2
    gathered = {}
    for chunk in (1, 0):
        (own,) = call(
            lambda *refs, c=chunk: finish_kernel(
                local_levels + early, levels, c * chunk_rows, *refs
            ),
            [((chunk_rows, width), BF16)],
            (run, queries, weight, gain, *reads[early:]),
            [VMEM] * (4 + len(reads) - early),
            2 * chunk_rows * width * DH * 2,
            2**20,
            "finish",
        )
        half = chunk_rows // 2
        left = shift(own, "head", lambda i: (i + 1) % group)
        right = shift(own, "head", lambda i: (i - 1) % group)
        far_left = shift(left[:half], "head", lambda i: (i + 1) % group)
        far_right = shift(right[half:], "head", lambda i: (i - 1) % group)
        gathered[chunk] = (own, left, right, far_left, far_right)
    w_parts = [
        lax.dynamic_slice(w_qkv, (0, part * model + head * width), (model, width))
        for part in range(3)
    ]
    out = {}
    for chunk in (1, 0):
        out[chunk] = call(
            lambda *refs, c=chunk: project_kernel(c, *refs),
            [((chunk_rows, width), BF16)] * 3 + [((BLOCK, model), BF16)],
            (info, *gathered[chunk], *res, w_out, norm_gain.reshape(1, model), *w_parts),
            [SMEM] + [VMEM] * 14,
            2 * chunk_rows * model * (model + 3 * width),
            2**23,
            "project",
            vmem=32,
        )
    hidden = jnp.where(head >= 2, out[1][3], out[0][3])
    tail = jnp.concatenate([out[1][1][-BLOCK:], out[1][2][-BLOCK:]], 1)
    before = shift(tail, "ctx", lambda i: i + 1)
    attended = []
    for chunk in (0, 1):
        q, k, v, _ = out[chunk]
        if chunk:
            k_before, v_before = out[0][1], out[0][2]
        else:
            k_before, v_before = before[:, :width], before[:, width:]
        (block,) = call(
            lambda *refs, c=chunk: attend_kernel(c == 0, *refs),
            [((chunk_rows, width), BF16)],
            (info, q, k, v, k_before, v_before),
            [SMEM] + [VMEM] * 5,
            4 * chunk_rows * 512 * width,
            2**20,
            "attend",
        )
        attended.append(block)
    return hidden, jnp.concatenate(attended, 0)


def solution(mesh):
    in_specs = (
        P("ctx", "head"),
        P("ctx", "head"),
        P("ctx", "head"),
        P("ctx"),
        P(None, "head", None),
        P("head"),
        P(("ctx", "head"), None),
        P(),
        P(),
        P(),
        P(),
    )
    out_specs = (P(("ctx", "head"), None), P("ctx", "head"))
    return jax.shard_map(
        per_device, mesh=mesh, in_specs=in_specs, out_specs=out_specs, check_vma=False
    )
```
